32 devices in a mesh: req: 4 (over z), mlp: 8 (over y, x, core).
Axes of the slice: x: 2, y: 2, z: 4, core: 2. Of those that a mesh axis runs over, the one named last changes fastest.
Arguments:
- tokens: bfloat16 [2048, 5120], P(('req', 'mlp')), may hold values from -6 to 6
- norm_scale: float32 [5120], replicated, may hold values from 0.25 to 1.75
- gate_matrix: bfloat16 [5120, 14336], P(None, 'mlp'), may hold values from -0.078125 to 0.078125
- up_matrix: bfloat16 [5120, 14336], P(None, 'mlp'), may hold values from -0.078125 to 0.078125
- down_matrix: bfloat16 [14336, 5120], P('mlp', 'req'), may hold values from -0.046875 to 0.046875
- adapter_down_maps: bfloat16 [8, 32, 5120], P('mlp'), may hold values from -0.078125 to 0.078125
- adapter_gate_up_out: bfloat16 [2, 128, 14336], P(None, None, 'mlp'), may hold values from -1.5 to 1.5
- adapter_down_proj_in: bfloat16 [128, 14336], P(None, 'mlp'), may hold values from -0.046875 to 0.046875
- adapter_down_proj_out: bfloat16 [128, 5120], replicated, may hold values from -1.5 to 1.5
- token_adapters: int32 [2048, 1], P(('req', 'mlp')), may hold values from 0 to 7; in each aligned block of 64 rows (0 to 63, 64 to 127, ...) at most 16 rows name the same one
Outputs:
- mixed: bfloat16 [2048, 5120], P(('req', 'mlp'))
The draws below stay inside these ranges and needn't reach their ends.
Inputs may be any that keep to these rules, and one draw needn't show every extreme that they name: `token_adapters`: among the 64 rows of one device no adapter is named by more than 16 rows, and in every draw some device has an adapter named by exactly 16 of its rows.
All inputs are finite; a program needn't handle non-finite values.
Results may differ from the reference program's by a relative error of at most 0.013.
Values may be sent and summed in bfloat16 or wider, within the bound.
A program may use at most 192 MiB of HBM per device.

```python
import math
import jax
import jax.numpy as jnp
import numpy as np
from jax import lax

MODEL_DIM = 5120
HIDDEN_UNITS = 14336
ADAPTER_RANK = 16
TOK_DEV = 64
CAP = 16
ADAPTER_COUNT = 8
TOKENS = 2048
N_REQ = 4
N_MLP = 8


def level_of(key, dims, split, low, high):
    gain, own = 1.0, jax.random.fold_in(key, 6)
    for axis_at, blocks in split:
        draws = jnp.exp(jax.random.uniform(jax.random.fold_in(own, axis_at), (blocks,), jnp.float32, low / len(split), high / len(split)))
        gain = gain * jnp.repeat(draws, dims[axis_at] // blocks).reshape([-1 if axis == axis_at else 1 for axis in range(len(dims))])
    return gain


def assign_block(key, own, number, rows, amount, top, reach, slope):
    ranking = jax.random.permutation(key, amount)
    packed, usual = shares(amount, rows * top, reach, slope, True), shares(amount, rows * top, reach, slope, False)
    places = jnp.arange(amount)

    def named(lengths, rotation):
        used = int((lengths > 0).sum())
        fixed = max(1, used // 4)
        moved = fixed + (places - fixed + rotation * (used - fixed)) % max(1, amount - fixed)
        return jnp.zeros((amount,), jnp.int32).at[ranking[jnp.where(places < fixed, places, moved)]].set(jnp.asarray(lengths, jnp.int32))

    lengths = jnp.where(number % 4 == 0, named(packed, number // 4), named(usual, number - number // 4 - 1))
    mixed = jax.random.permutation(jax.random.fold_in(own, 3), amount)
    giver, receiver = mixed[0:amount // 2 * 2:2], mixed[1:amount // 2 * 2:2]
    room = jnp.minimum(lengths[giver] - 1, reach - lengths[receiver]) // 2
    room = jnp.where((giver == ranking[0]) | (receiver == ranking[0]) | (lengths[receiver] == 0), 0, jnp.maximum(room, 0))
    moved = jax.random.randint(jax.random.fold_in(own, 4), (amount // 2,), 0, 1 << 20) % (room + 1)
    lengths = lengths.at[giver].add(-moved).at[receiver].add(moved)
    labels = jnp.searchsorted(jnp.cumsum(lengths), jnp.arange(rows * top), side="right").astype(jnp.int32)
    grid = labels.reshape(top, rows).T
    grid = grid[jax.random.permutation(jax.random.fold_in(own, 1), rows)]
    rotation = jax.random.randint(jax.random.fold_in(own, 2), (rows, 1), 0, top)
    return jnp.take_along_axis(grid, (jnp.arange(top)[None, :] + rotation) % top, axis=1)


def shares(number_of, total, bound, lean, full):
    loads = [(1 << 20) // math.isqrt(standing ** lean) + 1 for standing in range(1, number_of + 1)]
    largest = bound if full else min(bound, max(-(-total // number_of), total * loads[0] // sum(loads)))
    least = 1 if total - largest >= number_of - 1 else 0
    given, spare = [largest] + [least] * (number_of - 1), total - largest - least * (number_of - 1)
    while spare > 0:
        movable = [i for i in range(1, number_of) if given[i] < largest] or [i for i in range(1, number_of) if given[i] < bound]
        mass, budget = sum([loads[i] for i in movable]), spare
        for i in movable:
            more = min(bound - given[i], max(1, budget * loads[i] // mass), spare)
            given[i] = given[i] + more
            spare = spare - more
    return np.array(given)


def gaussian(stream_key, shape, scale, most, split=(), kind=jnp.bfloat16):
    values = scale * jax.random.normal(stream_key, shape, jnp.float32)
    if split:
        values = values * level_of(stream_key, shape, split, -0.22, 0.18)
    return jnp.clip(values, -most, most).astype(kind)


def setup_inputs(seed: int = 0) -> dict:
    seeds = jax.random.split(jax.random.key(seed), 11)
    tokens = gaussian(seeds[0], (TOKENS, MODEL_DIM), 1.0, 6.0, ((0, 32),))
    norm_scale = jnp.clip(1.0 + 0.15 * jax.random.normal(seeds[1], (MODEL_DIM,), jnp.float32), 0.25, 1.75)
    gate_matrix = gaussian(seeds[2], (MODEL_DIM, HIDDEN_UNITS), MODEL_DIM ** -0.5, 0.078125, ((1, 8),))
    up_matrix = gaussian(seeds[3], (MODEL_DIM, HIDDEN_UNITS), MODEL_DIM ** -0.5, 0.078125, ((1, 8),))
    down_matrix = gaussian(seeds[4], (HIDDEN_UNITS, MODEL_DIM), HIDDEN_UNITS ** -0.5, 0.046875, ((0, 8), (1, 4)))
    adapter_down_maps = gaussian(seeds[5], (ADAPTER_COUNT, 2 * ADAPTER_RANK, MODEL_DIM), MODEL_DIM ** -0.5, 0.078125, ((0, 8),))
    adapter_gate_up_out = gaussian(seeds[6], (2, ADAPTER_COUNT * ADAPTER_RANK, HIDDEN_UNITS), ADAPTER_RANK ** -0.5, 1.5, ((2, 8),))
    adapter_down_proj_in = gaussian(seeds[7], (ADAPTER_COUNT * ADAPTER_RANK, HIDDEN_UNITS), HIDDEN_UNITS ** -0.5, 0.046875, ((1, 8),))
    adapter_down_proj_out = gaussian(seeds[8], (ADAPTER_COUNT * ADAPTER_RANK, MODEL_DIM), ADAPTER_RANK ** -0.5, 1.5)
    token_adapters_keys = jax.random.split(jax.random.fold_in(seeds[9], 1), TOKENS // TOK_DEV)
    token_adapters_turns = jax.random.permutation(jax.random.fold_in(seeds[9], 3), TOKENS // TOK_DEV)
    token_adapters = jax.vmap(lambda own, number: assign_block(jax.random.fold_in(seeds[9], 2), own, number, TOK_DEV, ADAPTER_COUNT, 1, CAP, 2))(token_adapters_keys, token_adapters_turns).reshape((TOKENS, 1))
    return {"tokens": tokens, "norm_scale": norm_scale, "gate_matrix": gate_matrix, "up_matrix": up_matrix, "down_matrix": down_matrix, "adapter_down_maps": adapter_down_maps, "adapter_gate_up_out": adapter_gate_up_out, "adapter_down_proj_in": adapter_down_proj_in, "adapter_down_proj_out": adapter_down_proj_out, "token_adapters": token_adapters}


EPS = 1e-06

def normalize(tokens, norm_scale):
    widened = tokens.astype(jnp.float32)
    mean_square = lax.optimization_barrier(jnp.mean(widened * widened, axis=-1, keepdims=True))
    return (widened * lax.rsqrt(mean_square + EPS) * norm_scale.astype(jnp.float32)).astype(jnp.bfloat16)

def reference(tokens, norm_scale, gate_matrix, up_matrix, down_matrix, adapter_down_maps, adapter_gate_up_out, adapter_down_proj_in, adapter_down_proj_out, token_adapters):
    normed_input = normalize(tokens, norm_scale)
    adapter_lookup = token_adapters[:, 0]
    selector = adapter_lookup[:, None] == jnp.arange(ADAPTER_COUNT, dtype=jnp.int32)[None, :]
    projected_rows = jnp.dot(normed_input, adapter_down_maps.reshape(ADAPTER_COUNT * 2 * ADAPTER_RANK, MODEL_DIM).T, preferred_element_type=jnp.float32)
    projected_rows = projected_rows.reshape(TOKENS, ADAPTER_COUNT, 2 * ADAPTER_RANK)
    ranks = lax.optimization_barrier(jnp.sum(jnp.where(selector[:, :, None], projected_rows, jnp.float32(0.0)), axis=1)).astype(jnp.bfloat16)
    spread = jnp.where(selector[:, :, None], ranks[:, None, :], jnp.zeros((), jnp.bfloat16))
    gate_rank_values = spread[:, :, :ADAPTER_RANK].reshape(TOKENS, ADAPTER_COUNT * ADAPTER_RANK)
    up_rank_values = spread[:, :, ADAPTER_RANK:].reshape(TOKENS, ADAPTER_COUNT * ADAPTER_RANK)
    picker = jnp.repeat(selector, ADAPTER_RANK, axis=1)
    hidden_slice = HIDDEN_UNITS // N_MLP
    group_rows = TOKENS // N_REQ

    def one_group(group_items):
        grouped_tokens, gate_portion, up_portion, group_picker = group_items
        gate_total = jnp.dot(grouped_tokens, gate_matrix, preferred_element_type=jnp.float32) + jnp.dot(gate_portion, adapter_gate_up_out[0], preferred_element_type=jnp.float32)
        up_total = jnp.dot(grouped_tokens, up_matrix, preferred_element_type=jnp.float32) + jnp.dot(up_portion, adapter_gate_up_out[1], preferred_element_type=jnp.float32)
        hidden_state = (jax.nn.silu(gate_total) * up_total).astype(jnp.bfloat16)

        def add_block(running, block_index):
            down_total, total_rank = running
            leading_unit = (block_index * hidden_slice).astype(jnp.int32)
            hidden_block = lax.dynamic_slice_in_dim(hidden_state, leading_unit, hidden_slice, 1)
            down_block = lax.dynamic_slice_in_dim(down_matrix, leading_unit, hidden_slice, 0)
            adapter_slice = lax.dynamic_slice_in_dim(adapter_down_proj_in, leading_unit, hidden_slice, 1)
            down_term = jnp.dot(hidden_block, down_block, preferred_element_type=jnp.float32)
            rank_term = lax.dot_general(hidden_block, adapter_slice, (((1,), (1,)), ((), ())), preferred_element_type=jnp.float32)
            rank_term = jnp.where(group_picker, rank_term, jnp.float32(0.0))
            down_total = down_total + lax.optimization_barrier(down_term.astype(jnp.bfloat16)).astype(jnp.float32)
            total_rank = total_rank + lax.optimization_barrier(rank_term.astype(jnp.bfloat16)).astype(jnp.float32)
            return ((down_total, total_rank), None)
        start_sums = (jnp.zeros((group_rows, MODEL_DIM), jnp.float32), jnp.zeros((group_rows, ADAPTER_COUNT * ADAPTER_RANK), jnp.float32))
        (down_total, total_rank), _ = lax.scan(add_block, start_sums, jnp.arange(N_MLP, dtype=jnp.int32))
        return (down_total, total_rank)
    projected_down, rank_sum = lax.map(one_group, (normed_input.reshape(N_REQ, group_rows, MODEL_DIM), gate_rank_values.reshape(N_REQ, group_rows, ADAPTER_COUNT * ADAPTER_RANK), up_rank_values.reshape(N_REQ, group_rows, ADAPTER_COUNT * ADAPTER_RANK), picker.reshape(N_REQ, group_rows, ADAPTER_COUNT * ADAPTER_RANK)))
    projected_down = projected_down.reshape(TOKENS, MODEL_DIM)
    down_rank_values = rank_sum.reshape(TOKENS, ADAPTER_COUNT * ADAPTER_RANK).astype(jnp.bfloat16)
    adapter_down_term = jnp.dot(down_rank_values, adapter_down_proj_out, preferred_element_type=jnp.float32)
    return (tokens.astype(jnp.float32) + projected_down + adapter_down_term).astype(jnp.bfloat16)
```

```python
import jax
import jax.numpy as jnp
from jax import lax
from jax.sharding import PartitionSpec as P

CAP = 16


EPS = 1e-06


def normalize(tokens, norm_scale):
    widened = tokens.astype(jnp.float32)
    mean_square = jnp.mean(widened * widened, axis=-1, keepdims=True)
    return (widened * lax.rsqrt(mean_square + EPS) * norm_scale).astype(jnp.bfloat16)


def rank_routed(normed_input, adapter_lookup, adapter_down_maps, owner_list):
    capacity = CAP
    chosen = (adapter_lookup[:, None] == jnp.arange(owner_list, dtype=jnp.int32)[None, :]).astype(
        jnp.int32
    )
    earlier = jnp.cumsum(chosen, axis=0) - chosen
    slot_of = jnp.sum(earlier * chosen, axis=1)
    target = adapter_lookup * capacity + slot_of
    dispatch = (
        jnp.arange(owner_list * capacity, dtype=jnp.int32)[:, None] == target[None, :]
    ).astype(jnp.bfloat16)
    outgoing = jnp.dot(dispatch, normed_input, preferred_element_type=jnp.float32).astype(
        jnp.bfloat16
    )
    outgoing = outgoing.reshape(owner_list, capacity, normed_input.shape[1])
    owner_table = adapter_down_maps[0]
    produced = jnp.einsum(
        "nkd,rd->nkr",
        lax.all_to_all(outgoing, "mlp", split_axis=0, concat_axis=0, tiled=True),
        owner_table,
        preferred_element_type=jnp.float32,
    ).astype(jnp.bfloat16)
    returned = lax.all_to_all(produced, "mlp", split_axis=0, concat_axis=0, tiled=True)
    returned = returned.reshape(owner_list * capacity, returned.shape[2])
    return lax.dot_general(
        dispatch, returned, (((0,), (0,)), ((), ())), preferred_element_type=jnp.float32
    ).astype(jnp.bfloat16)


def per_device(
    tokens,
    norm_scale,
    gate_matrix,
    up_matrix,
    down_matrix,
    adapter_down_maps,
    adapter_gate_up_out,
    adapter_down_proj_in,
    adapter_down_proj_out,
    token_adapters,
):
    owner_list = lax.axis_size("mlp")
    rank_span = adapter_down_maps.shape[1]
    half_rank = rank_span // 2
    normed_input = normalize(tokens, norm_scale)
    adapter_lookup = token_adapters[:, 0]
    gathered = lax.all_gather(normed_input, "mlp", axis=0, tiled=True)
    group_of = lax.all_gather(adapter_lookup, "mlp", axis=0, tiled=True)
    group_rows = gathered.shape[0]
    selector = group_of[:, None] == jnp.arange(owner_list, dtype=jnp.int32)[None, :]
    zero_half = jnp.zeros((), jnp.bfloat16)
    rank_per_token = rank_routed(normed_input, adapter_lookup, adapter_down_maps, owner_list)
    rank_rows = lax.all_gather(rank_per_token, "mlp", axis=0, tiled=True)
    spread = jnp.where(selector[:, :, None], rank_rows[:, None, :], zero_half)
    gate_rank_values = spread[:, :, :half_rank].reshape(group_rows, owner_list * half_rank)
    up_rank_values = spread[:, :, half_rank:].reshape(group_rows, owner_list * half_rank)
    gate_total = jnp.dot(gathered, gate_matrix, preferred_element_type=jnp.float32) + jnp.dot(
        gate_rank_values, adapter_gate_up_out[0], preferred_element_type=jnp.float32
    )
    up_total = jnp.dot(gathered, up_matrix, preferred_element_type=jnp.float32) + jnp.dot(
        up_rank_values, adapter_gate_up_out[1], preferred_element_type=jnp.float32
    )
    hidden_state = (jax.nn.silu(gate_total) * up_total).astype(jnp.bfloat16)
    rank_term = lax.dot_general(
        hidden_state,
        adapter_down_proj_in,
        (((1,), (1,)), ((), ())),
        preferred_element_type=jnp.float32,
    )
    picker = jnp.repeat(selector, half_rank, axis=1)
    rank_term = jnp.where(picker, rank_term, jnp.float32(0.0))
    req_count = lax.axis_size("req")
    token_rows = tokens.shape[0]
    columns = down_matrix.shape[1]
    hidden_everywhere = lax.all_gather(hidden_state, "req", axis=0, tiled=True)
    down_term = jnp.dot(
        hidden_everywhere, down_matrix, preferred_element_type=jnp.float32
    ).astype(jnp.bfloat16)
    down_term = down_term.reshape(req_count, owner_list, token_rows, columns)
    down_term = down_term.transpose(1, 0, 2, 3).reshape(-1, columns)
    projected_down = lax.psum_scatter(down_term, "mlp", scatter_dimension=0, tiled=True)
    projected_down = lax.all_to_all(
        projected_down, "req", split_axis=0, concat_axis=1, tiled=True
    ).astype(jnp.float32)
    total_rank = lax.psum_scatter(
        rank_term.astype(jnp.bfloat16), "mlp", scatter_dimension=0, tiled=True
    )
    adapter_down_term = jnp.dot(
        total_rank, adapter_down_proj_out, preferred_element_type=jnp.float32
    )
    return (tokens.astype(jnp.float32) + projected_down + adapter_down_term).astype(jnp.bfloat16)


def solution(mesh):
    return jax.shard_map(
        per_device,
        mesh=mesh,
        in_specs=(
            P(("req", "mlp"), None),
            P(),
            P(None, "mlp"),
            P(None, "mlp"),
            P("mlp", "req"),
            P("mlp", None, None),
            P(None, None, "mlp"),
            P(None, "mlp"),
            P(),
            P(("req", "mlp"), None),
        ),
        out_specs=P(("req", "mlp"), None),
        check_vma=False,
    )
```

```python
import functools

import jax
import jax.numpy as jnp
from jax import lax
from jax.experimental import pallas as pl
from jax.experimental.pallas import tpu as pltpu
from jax.sharding import PartitionSpec as P

EPS = 1e-06
MESH = pl.DeviceIdType.MESH
F32 = jnp.float32
BF16 = jnp.bfloat16


def tile_of(width):
    return 256 if width % 256 == 0 else 128


def block_kernel(
    n_req,
    n_mlp,
    tokens,
    scale,
    names,
    gate_hbm,
    up_hbm,
    down_hbm,
    maps,
    ups,
    downs_in,
    downs_out,
    out,
    parts,
    x_all,
    a_all,
    w_gate,
    w_up,
    w_down,
    hid,
    acc,
    piece,
    z_in,
    rk_out,
    rk_in,
    w_sem,
    d_sem,
    c_sem,
    a_send,
    a_recv,
    x_send,
    x_recv,
    h_send,
    h_recv,
    p_send,
    p_recv,
    k_send,
    k_recv,
    e_send,
    e_recv,
):
    r = lax.axis_index("req")
    m = lax.axis_index("mlp")
    rows, dim = tokens.shape
    hidden = gate_hbm.shape[1]
    columns = down_hbm.shape[1]
    span = maps.shape[0]
    half = span // 2
    bits = n_mlp.bit_length() - 1
    tile = tile_of(hidden)
    tiles = hidden // tile
    group = n_req * rows

    def flip(index, bit):
        power = 1 << bit
        return index + power * (1 - 2 * ((index // power) % 2))

    def peer(slot):
        index = m
        for stage in range(bits):
            if (slot >> stage) & 1:
                index = flip(index, (stage + 1) % bits)
        return index

    def weight_copies(t):
        at = pl.ds(pl.multiple_of(t * tile, tile), tile)
        return (
            pltpu.make_async_copy(gate_hbm.at[:, at], w_gate.at[:, at], w_sem.at[0, t]),
            pltpu.make_async_copy(up_hbm.at[:, at], w_up.at[:, at], w_sem.at[1, t]),
        )

    for t in range(tiles):
        for copy in weight_copies(t):
            copy.start()
    down_copy = pltpu.make_async_copy(down_hbm, w_down, d_sem)
    down_copy.start()

    barrier = pltpu.get_barrier_semaphore()
    for slot in range(1, n_mlp):
        pl.semaphore_signal(barrier, inc=1, device_id=(r, peer(slot)), device_id_type=MESH)
    for step in range(1, n_req):
        pl.semaphore_signal(
            barrier, inc=1, device_id=((r + step) % n_req, m), device_id_type=MESH
        )
    pl.semaphore_wait(barrier, n_mlp - 1 + n_req - 1)

    def remote(src, dst, send, recv, device):
        return pltpu.make_async_remote_copy(
            src_ref=src,
            dst_ref=dst,
            send_sem=send,
            recv_sem=recv,
            device_id=device,
            device_id_type=MESH,
        )

    own_maps = pl.ds(pl.multiple_of(m * span, span), span)
    map_copies = [
        remote(maps, a_all.at[own_maps, :], a_send.at[s], a_recv.at[s], (r, peer(s)))
        for s in range(1, n_mlp)
    ]
    for copy in map_copies:
        copy.start()
    a_all[own_maps, :] = maps[...]

    def norm_step(i, carry):
        at = pl.ds(pl.multiple_of(i * 16, 16), 16)
        wide = tokens[at, :].astype(F32)
        mean_square = jnp.mean(wide * wide, axis=-1, keepdims=True)
        x_all[at, 0:dim] = (wide * lax.rsqrt(mean_square + EPS) * scale[...]).astype(BF16)
        x_all[at, dim : dim + 128] = jnp.broadcast_to(
            names[at, :].astype(F32), (16, 128)
        ).astype(BF16)
        return carry

    lax.fori_loop(0, rows // 16, norm_step, 0)

    def gather_copy(stage):
        size = rows << stage
        return remote(
            x_all.at[pl.ds(0, size), :],
            x_all.at[pl.ds(size, size), :],
            x_send.at[stage],
            x_recv.at[stage],
            (r, flip(m, (stage + 1) % bits)),
        )

    gather_copy(0).start()
    for copy in map_copies:
        copy.wait_recv()

    def hop(way, step, slot):
        at = pl.ds(slot * rows, rows)
        sign = 1 if way == 0 else -1
        block = r - sign * (step - 1)
        ok = (block >= 0) & (block <= n_req - 1) & (r + sign >= 0) & (r + sign <= n_req - 1)

        def make():
            return remote(
                hid.at[block, at, :],
                hid.at[block, at, :],
                h_send.at[way, step - 1, slot],
                h_recv.at[way, step - 1, slot],
                (r + sign, m),
            )

        return ok, make

    def hop_start(way, step, slot):
        ok, make = hop(way, step, slot)

        @pl.when(ok)
        def _():
            make().start()

    def hop_arrival(way, step, slot):
        at = pl.ds(slot * rows, rows)
        sign = 1 if way == 0 else -1
        block = r - sign * step

        @pl.when((block >= 0) & (block <= n_req - 1))
        def _():
            remote(
                hid.at[block, at, :],
                hid.at[block, at, :],
                h_send.at[way, step - 1, slot],
                h_recv.at[way, step - 1, slot],
                (r - sign, m),
            ).wait_recv()

    def tick(k):
        for step in range(n_req - 1, 0, -1):
            slot = k - step
            if 0 <= slot < n_mlp:
                for way in (0, 1):
                    hop_arrival(way, step, slot)
                    if step < n_req - 1:
                        hop_start(way, step + 1, slot)

    def rank_copy(slot):
        return remote(
            rk_out.at[slot], rk_in.at[slot], k_send.at[slot], k_recv.at[slot], (r, peer(slot))
        )

    def compute(first, count, wait):
        size = count * rows
        at = pl.ds(first * rows, size)
        normed = x_all[at, 0:dim]
        adapter = x_all[at, dim : dim + 128].astype(F32)[:, 0:1]
        ranks = lax.dot_general(
            normed, a_all[...], (((1,), (1,)), ((), ())), preferred_element_type=F32
        )
        lane = lax.broadcasted_iota(jnp.int32, ranks.shape, 1)
        mine = adapter == (lane // span).astype(F32)
        low = (lane // half) % 2 == 0
        gate_ranks = jnp.where(mine & low, ranks, 0.0).astype(BF16)
        up_ranks = jnp.where(mine & jnp.logical_not(low), ranks, 0.0).astype(BF16)

        def step(t, carry):
            if wait:
                for copy in weight_copies(t):
                    copy.wait()
            cols = pl.ds(pl.multiple_of(t * tile, tile), tile)
            table = ups[:, cols]
            gate_sum = jnp.dot(
                x_all[at, 0:dim], w_gate[:, cols], preferred_element_type=F32
            ) + jnp.dot(gate_ranks, table, preferred_element_type=F32)
            up_sum = jnp.dot(
                x_all[at, 0:dim], w_up[:, cols], preferred_element_type=F32
            ) + jnp.dot(up_ranks, table, preferred_element_type=F32)
            value = gate_sum / (1.0 + jnp.exp(-gate_sum)) * up_sum
            hid[r, at, cols] = value.astype(BF16)
            return carry

        lax.fori_loop(0, tiles, step, 0)
        for slot in range(first, first + count):
            hop_start(0, 1, slot)
            hop_start(1, 1, slot)
        terms = lax.dot_general(
            hid[r, at, :], downs_in[...], (((1,), (1,)), ((), ())), preferred_element_type=F32
        )
        lane = lax.broadcasted_iota(jnp.int32, terms.shape, 1)
        terms = jnp.where(adapter == (lane // half).astype(F32), terms, 0.0).astype(BF16)
        for slot in range(first, first + count):
            low_row = (slot - first) * rows
            term = terms[low_row : low_row + rows]
            if slot == 0:
                rk_in[0] = term
            else:
                rk_out[slot] = term
                rank_copy(slot).start()

    compute(0, 1, True)
    done = 0
    for stage in range(bits):
        gather_copy(stage).wait_recv()
        if stage + 1 < bits:
            gather_copy(stage + 1).start()
        compute(1 << stage, 1 << stage, False)
        if stage + 1 < bits:
            done = done + 1
            tick(done)

    down_copy.wait()
    narrow = tile_of(columns)

    def staging(slot):
        low_row = slot * group
        if low_row + group <= dim:
            return w_gate.at[pl.ds(low_row, group), pl.ds(0, columns)]
        low_row = (slot - dim // group) * group
        return w_up.at[pl.ds(low_row, group), pl.ds(0, columns)]

    def part_copy(slot):
        return remote(
            staging(slot), parts.at[slot], p_send.at[slot], p_recv.at[slot], (r, peer(slot))
        )

    def down(slot):
        place = staging(slot)
        at = pl.ds(slot * rows, rows)

        def step(t, carry):
            cols = pl.ds(pl.multiple_of(t * narrow, narrow), narrow)
            left = hid[:, at, :].reshape(group, hidden)
            term = jnp.dot(left, w_down[:, cols], preferred_element_type=F32).astype(BF16)
            if slot == 0:
                acc[:, cols] = term.astype(F32)
            else:
                place[:, cols] = term
            return carry

        lax.fori_loop(0, columns // narrow, step, 0)
        if slot > 0:
            part_copy(slot).start()

    def collect(slot):
        part_copy(slot).wait_recv()
        copy = pltpu.make_async_copy(parts.at[slot], piece, c_sem)
        copy.start()
        copy.wait()
        acc[...] += piece[...].astype(F32)

    finished = 0
    for k in range(done, n_mlp + n_req - 1):
        if k > done:
            tick(k)
        while finished <= k - (n_req - 1) and finished < n_mlp:
            down(finished)
            if finished >= 3:
                collect(finished - 2)
            finished += 1
    for slot in range(max(1, n_mlp - 2), n_mlp):
        collect(slot)

    piece[...] = acc[...].astype(BF16)

    def exchange(step):
        target = (r + step) % n_req
        return remote(
            piece.at[pl.ds(pl.multiple_of(target * rows, rows), rows), :],
            z_in.at[r],
            e_send.at[step],
            e_recv.at[step],
            (target, m),
        )

    for step in range(1, n_req):
        exchange(step).start()
    z_in[r] = piece[pl.ds(pl.multiple_of(r * rows, rows), rows), :]
    total = rk_in[0].astype(F32)
    for slot in range(1, n_mlp):
        rank_copy(slot).wait_recv()
        total = total + rk_in[slot].astype(F32)
    total = total.astype(BF16)
    for step in range(1, n_req):
        source = (r + n_req - step) % n_req
        remote(
            piece.at[pl.ds(0, rows), :],
            z_in.at[source],
            e_send.at[step],
            e_recv.at[step],
            (source, m),
        ).wait_recv()
    for c in range(n_req):
        cols = slice(c * columns, (c + 1) * columns)
        out[:, cols] = (
            tokens[:, cols].astype(F32)
            + z_in[c].astype(F32)
            + jnp.dot(total, downs_out[:, cols], preferred_element_type=F32)
        ).astype(BF16)

    for copy in map_copies:
        copy.wait_send()
    for stage in range(bits):
        gather_copy(stage).wait_send()
    for slot in range(n_mlp):
        for way in (0, 1):
            for step in range(1, n_req):
                ok, make = hop(way, step, slot)

                @pl.when(ok)
                def _():
                    make().wait_send()

    for slot in range(1, n_mlp):
        rank_copy(slot).wait_send()
        part_copy(slot).wait_send()
    for step in range(1, n_req):
        exchange(step).wait_send()


def per_device(
    tokens,
    norm_scale,
    gate_matrix,
    up_matrix,
    down_matrix,
    adapter_down_maps,
    adapter_gate_up_out,
    adapter_down_proj_in,
    adapter_down_proj_out,
    token_adapters,
):
    n_req, n_mlp = lax.axis_size("req"), lax.axis_size("mlp")
    rows, dim = tokens.shape
    hidden = gate_matrix.shape[1]
    columns = down_matrix.shape[1]
    span = adapter_down_maps.shape[1]
    half = span // 2
    ranks = adapter_down_proj_in.shape[0]
    bits = n_mlp.bit_length() - 1
    group = n_req * rows
    ups = adapter_gate_up_out.reshape(2, n_mlp, half, hidden)
    ups = ups.transpose(1, 0, 2, 3).reshape(n_mlp * span, hidden)
    vmem = pl.BlockSpec(memory_space=pltpu.VMEM)
    hbm = pl.BlockSpec(memory_space=pltpu.HBM)
    dma = pltpu.SemaphoreType.DMA
    out, _ = pl.pallas_call(
        functools.partial(block_kernel, n_req, n_mlp),
        out_shape=(
            jax.ShapeDtypeStruct((rows, dim), BF16),
            jax.ShapeDtypeStruct((n_mlp, group, columns), BF16),
        ),
        in_specs=[vmem, vmem, vmem, hbm, hbm, hbm, vmem, vmem, vmem, vmem],
        out_specs=(vmem, hbm),
        scratch_shapes=[
            pltpu.VMEM((n_mlp * rows, dim + 128), BF16),
            pltpu.VMEM((n_mlp * span, dim), BF16),
            pltpu.VMEM((dim, hidden), BF16),
            pltpu.VMEM((dim, hidden), BF16),
            pltpu.VMEM((hidden, columns), BF16),
            pltpu.VMEM((n_req, n_mlp * rows, hidden), BF16),
            pltpu.VMEM((group, columns), F32),
            pltpu.VMEM((group, columns), BF16),
            pltpu.VMEM((n_req, rows, columns), BF16),
            pltpu.VMEM((n_mlp, rows, ranks), BF16),
            pltpu.VMEM((n_mlp, rows, ranks), BF16),
            dma((2, hidden // tile_of(hidden))),
            dma,
            dma,
            dma((n_mlp,)),
            dma((n_mlp,)),
            dma((bits,)),
            dma((bits,)),
            dma((2, n_req - 1, n_mlp)),
            dma((2, n_req - 1, n_mlp)),
            dma((n_mlp,)),
            dma((n_mlp,)),
            dma((n_mlp,)),
            dma((n_mlp,)),
            dma((n_req,)),
            dma((n_req,)),
        ],
        compiler_params=pltpu.CompilerParams(
            collective_id=0, has_side_effects=True, vmem_limit_bytes=67043328
        ),
    )(
        tokens,
        norm_scale.reshape(1, dim),
        token_adapters,
        gate_matrix,
        up_matrix,
        down_matrix,
        adapter_down_maps[0],
        ups,
        adapter_down_proj_in,
        adapter_down_proj_out,
    )
    return out


def solution(mesh):
    return jax.shard_map(
        per_device,
        mesh=mesh,
        in_specs=(
            P(("req", "mlp"), None),
            P(),
            P(None, "mlp"),
            P(None, "mlp"),
            P("mlp", "req"),
            P("mlp", None, None),
            P(None, None, "mlp"),
            P(None, "mlp"),
            P(),
            P(("req", "mlp"), None),
        ),
        out_specs=P(("req", "mlp"), None),
        check_vma=False,
    )
```

```python
import functools

import jax
import jax.numpy as jnp
from jax import lax
from jax.experimental import pallas as pl
from jax.experimental.pallas import tpu as pltpu
from jax.sharding import PartitionSpec as P

EPS = 1e-06
MESH = pl.DeviceIdType.MESH
F32 = jnp.float32
BF16 = jnp.bfloat16


def tile_of(width):
    return 256 if width % 256 == 0 else 128


def block_kernel(
    n_req,
    n_mlp,
    tokens,
    scale,
    names,
    gate_hbm,
    up_hbm,
    down_hbm,
    maps,
    ups,
    downs_in,
    downs_out,
    out,
    parts,
    x_all,
    a_all,
    w_gate,
    w_up,
    w_down,
    hid,
    acc,
    piece,
    z_in,
    rk_out,
    rk_in,
    w_sem,
    d_sem,
    c_sem,
    a_send,
    a_recv,
    x_send,
    x_recv,
    h_send,
    h_recv,
    p_send,
    p_recv,
    k_send,
    k_recv,
    e_send,
    e_recv,
):
    r = lax.axis_index("req")
    m = lax.axis_index("mlp")
    rows, dim = tokens.shape
    hidden = gate_hbm.shape[1]
    columns = down_hbm.shape[1]
    span = maps.shape[0]
    half = span // 2
    bits = n_mlp.bit_length() - 1
    tile = tile_of(hidden)
    tiles = hidden // tile
    group = n_req * rows

    def flip(index, bit):
        power = 1 << bit
        return index + power * (1 - 2 * ((index // power) % 2))

    def peer(slot):
        index = m
        for stage in range(bits):
            if (slot >> stage) & 1:
                index = flip(index, (stage + 1) % bits)
        return index

    def weight_copies(t):
        at = pl.ds(pl.multiple_of(t * tile, tile), tile)
        return (
            pltpu.make_async_copy(gate_hbm.at[:, at], w_gate.at[:, at], w_sem.at[0, t]),
            pltpu.make_async_copy(up_hbm.at[:, at], w_up.at[:, at], w_sem.at[1, t]),
        )

    for t in range(tiles):
        for copy in weight_copies(t):
            copy.start()
    down_copy = pltpu.make_async_copy(down_hbm, w_down, d_sem)
    down_copy.start()

    barrier = pltpu.get_barrier_semaphore()
    for slot in range(1, n_mlp):
        pl.semaphore_signal(barrier, inc=1, device_id=(r, peer(slot)), device_id_type=MESH)
    for step in range(1, n_req):
        pl.semaphore_signal(
            barrier, inc=1, device_id=((r + step) % n_req, m), device_id_type=MESH
        )
    pl.semaphore_wait(barrier, n_mlp - 1 + n_req - 1)

    def remote(src, dst, send, recv, device):
        return pltpu.make_async_remote_copy(
            src_ref=src,
            dst_ref=dst,
            send_sem=send,
            recv_sem=recv,
            device_id=device,
            device_id_type=MESH,
        )

    own_maps = pl.ds(pl.multiple_of(m * span, span), span)
    map_copies = [
        remote(maps, a_all.at[own_maps, :], a_send.at[s], a_recv.at[s], (r, peer(s)))
        for s in range(1, n_mlp)
    ]
    for copy in map_copies:
        copy.start()
    a_all[own_maps, :] = maps[...]

    def norm_step(i, carry):
        at = pl.ds(pl.multiple_of(i * 16, 16), 16)
        wide = tokens[at, :].astype(F32)
        mean_square = jnp.mean(wide * wide, axis=-1, keepdims=True)
        x_all[at, 0:dim] = (wide * lax.rsqrt(mean_square + EPS) * scale[...]).astype(BF16)
        x_all[at, dim : dim + 128] = jnp.broadcast_to(
            names[at, :].astype(F32), (16, 128)
        ).astype(BF16)
        return carry

    lax.fori_loop(0, rows // 16, norm_step, 0)

    def gather_copy(stage):
        size = rows << stage
        return remote(
            x_all.at[pl.ds(0, size), :],
            x_all.at[pl.ds(size, size), :],
            x_send.at[stage],
            x_recv.at[stage],
            (r, flip(m, (stage + 1) % bits)),
        )

    gather_copy(0).start()
    for copy in map_copies:
        copy.wait_recv()

    def hop(way, step, slot):
        at = pl.ds(slot * rows, rows)
        sign = 1 if way == 0 else -1
        block = r - sign * (step - 1)
        ok = (block >= 0) & (block <= n_req - 1) & (r + sign >= 0) & (r + sign <= n_req - 1)

        def make():
            return remote(
                hid.at[block, at, :],
                hid.at[block, at, :],
                h_send.at[way, step - 1, slot],
                h_recv.at[way, step - 1, slot],
                (r + sign, m),
            )

        return ok, make

    def hop_start(way, step, slot):
        ok, make = hop(way, step, slot)

        @pl.when(ok)
        def _():
            make().start()

    def hop_arrival(way, step, slot):
        at = pl.ds(slot * rows, rows)
        sign = 1 if way == 0 else -1
        block = r - sign * step

        @pl.when((block >= 0) & (block <= n_req - 1))
        def _():
            remote(
                hid.at[block, at, :],
                hid.at[block, at, :],
                h_send.at[way, step - 1, slot],
                h_recv.at[way, step - 1, slot],
                (r - sign, m),
            ).wait_recv()

    middle = n_mlp // 2
    order = [*range(middle), *range(middle + 1, n_mlp), middle]

    def tick(k):
        for step in range(n_req - 1, 0, -1):
            if 0 <= k - step < n_mlp:
                slot = order[k - step]
                for way in (0, 1):
                    hop_arrival(way, step, slot)
                    if step < n_req - 1:
                        hop_start(way, step + 1, slot)

    def rank_copy(slot):
        return remote(
            rk_out.at[slot], rk_in.at[slot], k_send.at[slot], k_recv.at[slot], (r, peer(slot))
        )

    def compute(first, count, wait, ticks):
        size = count * rows
        at = pl.ds(first * rows, size)
        normed = x_all[at, 0:dim]
        adapter = x_all[at, dim : dim + 128].astype(F32)[:, 0:1]
        ranks = lax.dot_general(
            normed, a_all[...], (((1,), (1,)), ((), ())), preferred_element_type=F32
        )
        lane = lax.broadcasted_iota(jnp.int32, ranks.shape, 1)
        mine = adapter == (lane // span).astype(F32)
        low = (lane // half) % 2 == 0
        gate_ranks = jnp.where(mine & low, ranks, 0.0).astype(BF16)
        up_ranks = jnp.where(mine & jnp.logical_not(low), ranks, 0.0).astype(BF16)

        def step(t, carry):
            if wait:
                for copy in weight_copies(t):
                    copy.wait()
            cols = pl.ds(pl.multiple_of(t * tile, tile), tile)
            table = ups[:, cols]
            gate_sum = jnp.dot(
                x_all[at, 0:dim], w_gate[:, cols], preferred_element_type=F32
            ) + jnp.dot(gate_ranks, table, preferred_element_type=F32)
            up_sum = jnp.dot(
                x_all[at, 0:dim], w_up[:, cols], preferred_element_type=F32
            ) + jnp.dot(up_ranks, table, preferred_element_type=F32)
            value = gate_sum / (1.0 + jnp.exp(-gate_sum)) * up_sum
            hid[r, at, cols] = value.astype(BF16)
            return carry

        reached = 0
        for i, k in enumerate(ticks):
            limit = tiles * (i + 1) // (len(ticks) + 1)
            lax.fori_loop(reached, limit, step, 0)
            reached = limit
            tick(k)
        lax.fori_loop(reached, tiles, step, 0)
        for slot in order[first : first + count]:
            hop_start(0, 1, slot)
            hop_start(1, 1, slot)
        terms = lax.dot_general(
            hid[r, at, :], downs_in[...], (((1,), (1,)), ((), ())), preferred_element_type=F32
        )
        lane = lax.broadcasted_iota(jnp.int32, terms.shape, 1)
        terms = jnp.where(adapter == (lane // half).astype(F32), terms, 0.0).astype(BF16)
        for slot in range(first, first + count):
            low_row = (slot - first) * rows
            term = terms[low_row : low_row + rows]
            if slot == 0:
                rk_in[0] = term
            else:
                rk_out[slot] = term
                rank_copy(slot).start()

    gather_copy(0).wait_recv()
    gather_copy(1).start()
    compute(0, 2, True, ())
    done = 0
    for stage in range(1, bits):
        gather_copy(stage).wait_recv()
        if stage + 1 < bits:
            gather_copy(stage + 1).start()
        compute(1 << stage, 1 << stage, False, (done + 1, done + 2))
        done = done + 2

    down_copy.wait()
    narrow = tile_of(columns)

    def staging(slot):
        low_row = slot * group
        if low_row + group <= dim:
            return w_gate.at[pl.ds(low_row, group), pl.ds(0, columns)]
        low_row = (slot - dim // group) * group
        return w_up.at[pl.ds(low_row, group), pl.ds(0, columns)]

    def part_copy(slot):
        return remote(
            staging(slot), parts.at[slot], p_send.at[slot], p_recv.at[slot], (r, peer(slot))
        )

    def down(slot):
        place = staging(slot)
        at = pl.ds(slot * rows, rows)

        def step(t, carry):
            cols = pl.ds(pl.multiple_of(t * narrow, narrow), narrow)
            left = hid[:, at, :].reshape(group, hidden)
            term = jnp.dot(left, w_down[:, cols], preferred_element_type=F32).astype(BF16)
            if slot == 0:
                acc[:, cols] = term.astype(F32)
            else:
                place[:, cols] = term
            return carry

        lax.fori_loop(0, columns // narrow, step, 0)
        if slot > 0:
            part_copy(slot).start()

    def collect(slot):
        part_copy(slot).wait_recv()
        copy = pltpu.make_async_copy(parts.at[slot], piece, c_sem)
        copy.start()
        copy.wait()
        acc[...] += piece[...].astype(F32)

    finished = 0
    for k in range(done, n_mlp + n_req - 1):
        if k > done:
            tick(k)
        while finished <= k - (n_req - 1) and finished < n_mlp:
            down(order[finished])
            if finished >= 3:
                collect(order[finished - 2])
            finished += 1
    for slot in order[n_mlp - 2 :]:
        collect(slot)

    piece[...] = acc[...].astype(BF16)

    def exchange(step):
        target = (r + step) % n_req
        return remote(
            piece.at[pl.ds(pl.multiple_of(target * rows, rows), rows), :],
            z_in.at[r],
            e_send.at[step],
            e_recv.at[step],
            (target, m),
        )

    for step in range(1, n_req):
        exchange(step).start()
    z_in[r] = piece[pl.ds(pl.multiple_of(r * rows, rows), rows), :]
    total = rk_in[0].astype(F32)
    for slot in range(1, n_mlp):
        rank_copy(slot).wait_recv()
        total = total + rk_in[slot].astype(F32)
    total = total.astype(BF16)
    for step in range(1, n_req):
        source = (r + n_req - step) % n_req
        remote(
            piece.at[pl.ds(0, rows), :],
            z_in.at[source],
            e_send.at[step],
            e_recv.at[step],
            (source, m),
        ).wait_recv()
    for c in range(n_req):
        cols = slice(c * columns, (c + 1) * columns)
        out[:, cols] = (
            tokens[:, cols].astype(F32)
            + z_in[c].astype(F32)
            + jnp.dot(total, downs_out[:, cols], preferred_element_type=F32)
        ).astype(BF16)

    for copy in map_copies:
        copy.wait_send()
    for stage in range(bits):
        gather_copy(stage).wait_send()
    for slot in range(n_mlp):
        for way in (0, 1):
            for step in range(1, n_req):
                ok, make = hop(way, step, slot)

                @pl.when(ok)
                def _():
                    make().wait_send()

    for slot in range(1, n_mlp):
        rank_copy(slot).wait_send()
        part_copy(slot).wait_send()
    for step in range(1, n_req):
        exchange(step).wait_send()


def per_device(
    tokens,
    norm_scale,
    gate_matrix,
    up_matrix,
    down_matrix,
    adapter_down_maps,
    adapter_gate_up_out,
    adapter_down_proj_in,
    adapter_down_proj_out,
    token_adapters,
):
    n_req, n_mlp = lax.axis_size("req"), lax.axis_size("mlp")
    rows, dim = tokens.shape
    hidden = gate_matrix.shape[1]
    columns = down_matrix.shape[1]
    span = adapter_down_maps.shape[1]
    half = span // 2
    ranks = adapter_down_proj_in.shape[0]
    bits = n_mlp.bit_length() - 1
    group = n_req * rows
    ups = adapter_gate_up_out.reshape(2, n_mlp, half, hidden)
    ups = ups.transpose(1, 0, 2, 3).reshape(n_mlp * span, hidden)
    vmem = pl.BlockSpec(memory_space=pltpu.VMEM)
    hbm = pl.BlockSpec(memory_space=pltpu.HBM)
    dma = pltpu.SemaphoreType.DMA
    out, _ = pl.pallas_call(
        functools.partial(block_kernel, n_req, n_mlp),
        out_shape=(
            jax.ShapeDtypeStruct((rows, dim), BF16),
            jax.ShapeDtypeStruct((n_mlp, group, columns), BF16),
        ),
        in_specs=[vmem, vmem, vmem, hbm, hbm, hbm, vmem, vmem, vmem, vmem],
        out_specs=(vmem, hbm),
        scratch_shapes=[
            pltpu.VMEM((n_mlp * rows, dim + 128), BF16),
            pltpu.VMEM((n_mlp * span, dim), BF16),
            pltpu.VMEM((dim, hidden), BF16),
            pltpu.VMEM((dim, hidden), BF16),
            pltpu.VMEM((hidden, columns), BF16),
            pltpu.VMEM((n_req, n_mlp * rows, hidden), BF16),
            pltpu.VMEM((group, columns), F32),
            pltpu.VMEM((group, columns), BF16),
            pltpu.VMEM((n_req, rows, columns), BF16),
            pltpu.VMEM((n_mlp, rows, ranks), BF16),
            pltpu.VMEM((n_mlp, rows, ranks), BF16),
            dma((2, hidden // tile_of(hidden))),
            dma,
            dma,
            dma((n_mlp,)),
            dma((n_mlp,)),
            dma((bits,)),
            dma((bits,)),
            dma((2, n_req - 1, n_mlp)),
            dma((2, n_req - 1, n_mlp)),
            dma((n_mlp,)),
            dma((n_mlp,)),
            dma((n_mlp,)),
            dma((n_mlp,)),
            dma((n_req,)),
            dma((n_req,)),
        ],
        compiler_params=pltpu.CompilerParams(
            collective_id=0, has_side_effects=True, vmem_limit_bytes=67043328
        ),
    )(
        tokens,
        norm_scale.reshape(1, dim),
        token_adapters,
        gate_matrix,
        up_matrix,
        down_matrix,
        adapter_down_maps[0],
        ups,
        adapter_down_proj_in,
        adapter_down_proj_out,
    )
    return out


def solution(mesh):
    return jax.shard_map(
        per_device,
        mesh=mesh,
        in_specs=(
            P(("req", "mlp"), None),
            P(),
            P(None, "mlp"),
            P(None, "mlp"),
            P("mlp", "req"),
            P("mlp", None, None),
            P(None, None, "mlp"),
            P(None, "mlp"),
            P(),
            P(("req", "mlp"), None),
        ),
        out_specs=P(("req", "mlp"), None),
        check_vma=False,
    )
```
